32 devices in a mesh: shard: 4 (over x, core), context: 2 (over y), tensor: 4 (over z).
Axes of the slice: x: 2, y: 2, z: 4, core: 2. Of those that a mesh axis runs over, the one named last changes fastest.
Arguments:
- tokens: bfloat16 [4, 512, 1024], P('shard', 'context'), may hold values from -12 to 12
- cotangent: bfloat16 [4, 512, 1024], P('shard', 'context'), may hold values from -12 to 12
- query_weight: bfloat16 [1024, 1024], P(('shard', 'context'), 'tensor'), may hold values from -0.1875 to 0.1875
- key_weight: bfloat16 [1024, 1024], P(('shard', 'context'), 'tensor'), may hold values from -0.1875 to 0.1875
- value_weight: bfloat16 [1024, 1024], P(('shard', 'context'), 'tensor'), may hold values from -0.1875 to 0.1875
- output_weight: bfloat16 [1024, 1024], P(('shard', 'context'), 'tensor'), may hold values from -2.5 to 2.5
- query_bias: float32 [1024], P('tensor'), may hold values from -3 to 3
- value_bias: float32 [1024], P('tensor'), may hold values from -3 to 3
- output_bias: float32 [1024], replicated, may hold values from -3 to 3
- first_gain: float32 [1024], replicated, may hold values from 0.1 to 1.9
- first_shift: float32 [1024], replicated, may hold values from -2.5 to 2.5
- up_weight: bfloat16 [1024, 4096], P(('shard', 'context'), 'tensor'), may hold values from -0.1875 to 0.1875
- up_bias: float32 [4096], P('tensor'), may hold values from -3 to 3
- down_weight: bfloat16 [1024, 4096], P(('shard', 'context'), 'tensor'), may hold values from -0.09375 to 0.09375
- down_bias: float32 [1024], replicated, may hold values from -3 to 3
- second_gain: float32 [1024], replicated, may hold values from 0.1 to 1.9
- second_shift: float32 [1024], replicated, may hold values from -2.5 to 2.5
Outputs:
- layer_output: bfloat16 [4, 512, 1024], P('shard', 'context')
- input_grad: float32 [4, 512, 1024], P('shard', 'context')
- grad_query_weight: float32 [1024, 1024], P(('shard', 'context'), 'tensor')
- grad_key_weight: float32 [1024, 1024], P(('shard', 'context'), 'tensor')
- grad_value_weight: float32 [1024, 1024], P(('shard', 'context'), 'tensor')
- grad_output_weight: float32 [1024, 1024], P(('shard', 'context'), 'tensor')
- grad_query_bias: float32 [1024], P('tensor')
- grad_value_bias: float32 [1024], P('tensor')
- grad_output_bias: float32 [1024], replicated
- grad_first_gain: float32 [1024], replicated
- grad_first_shift: float32 [1024], replicated
- grad_up_weight: float32 [1024, 4096], P(('shard', 'context'), 'tensor')
- grad_up_bias: float32 [4096], P('tensor')
- grad_down_weight: float32 [1024, 4096], P(('shard', 'context'), 'tensor')
- grad_down_bias: float32 [1024], replicated
- grad_second_gain: float32 [1024], replicated
- grad_second_shift: float32 [1024], replicated
The draws below stay inside these ranges and needn't reach their ends.
All inputs are finite; a program needn't handle non-finite values.
Results may differ from the reference program's by a relative error of at most 0.028.
The reference program's roundings to bfloat16 on the way (of `query`, `keys`, `values`, `attended`, `first_round`, `active`, `back_two_round` and `grad_attended`) count: a program that leaves them out, or rounds other values in their place, can miss the bound.
Values may be sent and summed in bfloat16 or wider, within the bound.
A program may use at most 128 MiB of HBM per device.

```python
import jax
import jax.numpy as jnp
from jax import lax

D = 1024
HEADS = 16
DH = 64
FF = 4096
HD = 1024
LEN = 512
SEQS = 4


def draw_tokens(key, part):
    shape = (SEQS, LEN, D)
    base = jnp.clip(jax.random.normal(jax.random.fold_in(key, 17), shape, jnp.float32), -6.0, 6.0)
    return base.astype(jnp.bfloat16)


def draw_cotangent(key, part):
    shape = (SEQS, LEN, D)
    rows = jnp.arange(SEQS * LEN).astype(jnp.float32).reshape(SEQS, LEN, 1)
    ramp = 1.0 + 2.0 * rows / (SEQS * LEN - 1.0)
    base = jnp.clip(jax.random.normal(jax.random.fold_in(key, 23), shape, jnp.float32), -4.0, 4.0)
    return (base * ramp).astype(jnp.bfloat16)


def block_levels(own_key, extent, shards, least, high):
    loudness, own = 1.0, jax.random.fold_in(own_key, 6)
    for dim, shards_of in shards:
        draws = jnp.exp(jax.random.uniform(jax.random.fold_in(own, dim), (shards_of,), jnp.float32, least / len(shards), high / len(shards)))
        loudness = loudness * jnp.repeat(draws, extent[dim] // shards_of).reshape([-1 if axis == dim else 1 for axis in range(len(extent))])
    return loudness


def normal_values(own_key, shape, deviation, most, split=(), dtype=jnp.bfloat16):
    entries = deviation * jax.random.normal(own_key, shape, jnp.float32)
    if split:
        entries = entries * block_levels(own_key, shape, split, -0.22, 0.18)
    return jnp.clip(entries, -most, most).astype(dtype)


def setup_inputs(seed: int = 0) -> dict:
    key_list = jax.random.split(jax.random.key(seed), 18)
    return {
        "tokens": draw_tokens(jax.random.fold_in(key_list[17], 71), 0),
        "cotangent": draw_cotangent(jax.random.fold_in(key_list[17], 71), 0),
        "query_weight": normal_values(key_list[2], (D, HD), D ** -0.5, 0.1875, ((0, 8), (1, 4))),
        "key_weight": normal_values(key_list[3], (D, HD), D ** -0.5, 0.1875, ((0, 8), (1, 4))),
        "value_weight": normal_values(key_list[4], (D, HD), D ** -0.5, 0.1875, ((0, 8), (1, 4))),
        "output_weight": normal_values(key_list[5], (D, HD), ((2 * HD) // LEN + 1) ** -0.5, 2.5, ((0, 8), (1, 4))),
        "query_bias": normal_values(key_list[6], (HD,), 1.0, 3.0, ((0, 4),), jnp.float32),
        "value_bias": normal_values(key_list[7], (HD,), 1.0, 3.0, ((0, 4),), jnp.float32),
        "output_bias": normal_values(key_list[8], (D,), 1.0, 3.0, (), jnp.float32),
        "first_gain": jnp.clip(1.0 + 0.18 * jax.random.normal(key_list[9], (D,), jnp.float32), 0.1, 1.9),
        "first_shift": normal_values(key_list[10], (D,), 0.6, 2.5, (), jnp.float32),
        "up_weight": normal_values(key_list[11], (D, FF), D ** -0.5, 0.1875, ((0, 8), (1, 4))),
        "up_bias": normal_values(key_list[12], (FF,), 1.0, 3.0, ((0, 4),), jnp.float32),
        "down_weight": normal_values(key_list[13], (D, FF), FF ** -0.5, 0.09375, ((0, 8), (1, 4))),
        "down_bias": normal_values(key_list[14], (D,), 1.0, 3.0, (), jnp.float32),
        "second_gain": jnp.clip(1.0 + 0.18 * jax.random.normal(key_list[15], (D,), jnp.float32), 0.1, 1.9),
        "second_shift": normal_values(key_list[16], (D,), 0.6, 2.5, (), jnp.float32),
    }


epsilon = 1e-05
root_half = 0.7071067811865476
inverse_root_two_pi = 0.3989422804014327

def layer_norm(hidden, gain, shift):
    center = hidden - lax.optimization_barrier(jnp.mean(hidden, axis=-1, keepdims=True))
    inverse = lax.rsqrt(lax.optimization_barrier(jnp.mean(center * center, axis=-1, keepdims=True)) + epsilon)
    normed = center * inverse
    return (normed * gain + shift, normed, inverse)

def norm_backward(grad, normed, inverse, gain):
    scaled = grad * gain
    return (scaled - lax.optimization_barrier(jnp.mean(scaled, axis=-1, keepdims=True)) - normed * lax.optimization_barrier(jnp.mean(scaled * normed, axis=-1, keepdims=True))) * inverse

def gelu_value(values):
    return 0.5 * values * (1.0 + lax.erf(values * root_half))

def gelu_slope(values):
    return 0.5 * (1.0 + lax.erf(values * root_half)) + values * inverse_root_two_pi * jnp.exp(-0.5 * values * values)

def head_forward(operands):
    query_head, key_head, value_head = operands
    scores = jnp.dot(query_head, key_head.T, preferred_element_type=jnp.float32) * DH ** (-0.5)
    top = lax.optimization_barrier(jnp.max(scores, axis=1, keepdims=True))
    exponent = jnp.exp(scores - top)
    total = lax.optimization_barrier(jnp.sum(exponent, axis=1, keepdims=True))
    mixed = jnp.dot(exponent.astype(jnp.bfloat16), value_head, preferred_element_type=jnp.float32) / total
    return (mixed, (top + jnp.log(total))[:, 0])

def head_backward(operands):
    query_head, key_head, value_head, grad_head, logsum, delta = operands
    scale = DH ** (-0.5)
    scores = jnp.dot(query_head, key_head.T, preferred_element_type=jnp.float32) * scale
    probs = jnp.exp(scores - logsum[:, None])
    grad_probs = jnp.dot(grad_head, value_head.T, preferred_element_type=jnp.float32)
    grad_scores = (probs * (grad_probs - delta[:, None])).astype(jnp.bfloat16)
    grad_query = jnp.dot(grad_scores, key_head, preferred_element_type=jnp.float32) * scale
    grad_keys = jnp.dot(grad_scores.T, query_head, preferred_element_type=jnp.float32) * scale
    grad_values = jnp.dot(probs.astype(jnp.bfloat16).T, grad_head, preferred_element_type=jnp.float32)
    return (grad_query, grad_keys, grad_values)

def split_heads(matrix):
    return matrix.reshape(matrix.shape[0], HEADS, DH).transpose(1, 0, 2)

def merge_heads(stacked):
    return stacked.transpose(1, 0, 2).reshape(stacked.shape[1], HEADS * DH)

def sequence_pass(inputs, cotangent, params):
    query_weight, key_weight, value_weight, output_weight, query_bias, value_bias, output_bias, first_gain, first_shift, up_weight, up_bias, down_weight, down_bias, second_gain, second_shift = params
    query = (jnp.dot(inputs, query_weight, preferred_element_type=jnp.float32) + query_bias).astype(jnp.bfloat16)
    keys = jnp.dot(inputs, key_weight, preferred_element_type=jnp.float32).astype(jnp.bfloat16)
    values = (jnp.dot(inputs, value_weight, preferred_element_type=jnp.float32) + value_bias).astype(jnp.bfloat16)
    query_heads, key_heads, value_heads = (split_heads(query), split_heads(keys), split_heads(values))
    mixed, logsum = lax.map(head_forward, (query_heads, key_heads, value_heads))
    attended = merge_heads(mixed).astype(jnp.bfloat16)
    first_sum = inputs.astype(jnp.float32) + jnp.dot(attended, output_weight.T, preferred_element_type=jnp.float32) + output_bias
    first_out, normed_one, inverse_one = layer_norm(first_sum, first_gain, first_shift)
    first_round = first_out.astype(jnp.bfloat16)
    up = jnp.dot(first_round, up_weight, preferred_element_type=jnp.float32) + up_bias
    active = gelu_value(up).astype(jnp.bfloat16)
    second_sum = first_out + jnp.dot(active, down_weight.T, preferred_element_type=jnp.float32) + down_bias
    second_out, normed_two, inverse_two = layer_norm(second_sum, second_gain, second_shift)
    layer_output = second_out.astype(jnp.bfloat16)
    grad_out = cotangent.astype(jnp.float32)
    grad_second_gain = lax.optimization_barrier(jnp.sum(grad_out * normed_two, axis=0))
    grad_second_shift = lax.optimization_barrier(jnp.sum(grad_out, axis=0))
    back_two = norm_backward(grad_out, normed_two, inverse_two, second_gain)
    grad_down_bias = lax.optimization_barrier(jnp.sum(back_two, axis=0))
    back_two_round = back_two.astype(jnp.bfloat16)
    grad_down_weight = jnp.dot(back_two_round.T, active, preferred_element_type=jnp.float32)
    grad_up = jnp.dot(back_two_round, down_weight, preferred_element_type=jnp.float32) * gelu_slope(up)
    grad_up_bias = lax.optimization_barrier(jnp.sum(grad_up, axis=0))
    up_round = grad_up.astype(jnp.bfloat16)
    grad_up_weight = jnp.dot(first_round.T, up_round, preferred_element_type=jnp.float32)
    back_one_in = jnp.dot(up_round, up_weight.T, preferred_element_type=jnp.float32) + back_two
    grad_first_gain = lax.optimization_barrier(jnp.sum(back_one_in * normed_one, axis=0))
    grad_first_shift = lax.optimization_barrier(jnp.sum(back_one_in, axis=0))
    back_one = norm_backward(back_one_in, normed_one, inverse_one, first_gain)
    grad_output_bias = lax.optimization_barrier(jnp.sum(back_one, axis=0))
    back_one_round = back_one.astype(jnp.bfloat16)
    grad_output_weight = jnp.dot(back_one_round.T, attended, preferred_element_type=jnp.float32)
    grad_attended = jnp.dot(back_one_round, output_weight, preferred_element_type=jnp.float32).astype(jnp.bfloat16)
    grad_heads = split_heads(grad_attended)
    delta = lax.optimization_barrier(jnp.sum(grad_heads.astype(jnp.float32) * split_heads(attended).astype(jnp.float32), axis=2))
    grad_q, grad_k, grad_v = lax.map(head_backward, (query_heads, key_heads, value_heads, grad_heads, logsum, delta))
    grad_query, grad_keys, grad_values = (merge_heads(grad_q), merge_heads(grad_k), merge_heads(grad_v))
    grad_query_bias = lax.optimization_barrier(jnp.sum(grad_query, axis=0))
    grad_value_bias = lax.optimization_barrier(jnp.sum(grad_values, axis=0))
    query_round = grad_query.astype(jnp.bfloat16)
    keys_round = grad_keys.astype(jnp.bfloat16)
    values_round = grad_values.astype(jnp.bfloat16)
    grad_query_weight = jnp.dot(inputs.T, query_round, preferred_element_type=jnp.float32)
    grad_key_weight = jnp.dot(inputs.T, keys_round, preferred_element_type=jnp.float32)
    grad_value_weight = jnp.dot(inputs.T, values_round, preferred_element_type=jnp.float32)
    input_grad = jnp.dot(query_round, query_weight.T, preferred_element_type=jnp.float32) + jnp.dot(keys_round, key_weight.T, preferred_element_type=jnp.float32) + jnp.dot(values_round, value_weight.T, preferred_element_type=jnp.float32) + back_one
    grads = (grad_query_weight, grad_key_weight, grad_value_weight, grad_output_weight, grad_query_bias, grad_value_bias, grad_output_bias, grad_first_gain, grad_first_shift, grad_up_weight, grad_up_bias, grad_down_weight, grad_down_bias, grad_second_gain, grad_second_shift)
    return (layer_output, input_grad, grads)

def reference(tokens, cotangent, query_weight, key_weight, value_weight, output_weight, query_bias, value_bias, output_bias, first_gain, first_shift, up_weight, up_bias, down_weight, down_bias, second_gain, second_shift):
    params = (query_weight, key_weight, value_weight, output_weight, query_bias, value_bias, output_bias, first_gain, first_shift, up_weight, up_bias, down_weight, down_bias, second_gain, second_shift)
    initial = tuple((jnp.zeros(param.shape, jnp.float32) for param in params))

    def one_sequence(carry, pair):
        layer_output, input_grad, grads = sequence_pass(pair[0], pair[1], params)
        return (jax.tree.map(jnp.add, carry, grads), (layer_output, input_grad))
    totals, stacked = lax.scan(one_sequence, initial, (tokens, cotangent))
    return (stacked[0], stacked[1], totals[0], totals[1], totals[2], totals[3], totals[4], totals[5], totals[6], totals[7], totals[8], totals[9], totals[10], totals[11], totals[12], totals[13], totals[14])
```

```python
import jax
import jax.numpy as jnp
from jax import lax
from jax.sharding import PartitionSpec as P

DH = 64


epsilon = 1e-05
root_half = 0.7071067811865476
inverse_root_two_pi = 0.3989422804014327


def passed_along(shard, axis, by):
    size = lax.axis_size(axis)
    return lax.ppermute(shard, axis, [(i, (i + by) % size) for i in range(size)])


def layer_norm(hidden, gain, shift):
    center = hidden - jnp.mean(hidden, axis=-1, keepdims=True)
    inverse = lax.rsqrt(jnp.mean(center * center, axis=-1, keepdims=True) + epsilon)
    normed = center * inverse
    return (normed * gain + shift, normed, inverse)


def norm_backward(grad, normed, inverse, gain):
    scaled = grad * gain
    return (
        scaled
        - jnp.mean(scaled, axis=-1, keepdims=True)
        - normed * jnp.mean(scaled * normed, axis=-1, keepdims=True)
    ) * inverse


def gelu_value(values):
    return 0.5 * values * (1.0 + lax.erf(values * root_half))


def gelu_slope(values):
    return 0.5 * (1.0 + lax.erf(values * root_half)) + values * inverse_root_two_pi * jnp.exp(
        -0.5 * values * values
    )


def forward_total(partial_value):
    return lax.psum(partial_value.astype(jnp.bfloat16), "tensor").astype(jnp.float32)


def backward_total(partial_value):
    return lax.psum(partial_value.astype(jnp.bfloat16), "tensor").astype(jnp.float32)


def scattered(partial_value):
    return lax.psum_scatter(
        partial_value.astype(jnp.bfloat16), ("shard", "context"), scatter_dimension=0, tiled=True
    ).astype(jnp.float32)


def rotate_grads(stacked):
    return passed_along(stacked.astype(jnp.bfloat16), "context", 1).astype(stacked.dtype)


def shards(
    tokens,
    cotangent,
    query_weight,
    key_weight,
    value_weight,
    output_weight,
    query_bias,
    value_bias,
    output_bias,
    first_gain,
    first_shift,
    up_weight,
    up_bias,
    down_weight,
    down_bias,
    second_gain,
    second_shift,
):
    inputs = tokens[0]
    rows = inputs.shape[0]
    width = query_weight.shape[1]
    heads = width // DH
    scale = DH ** (-0.5)
    query_full, key_full, value_full, output_full = (
        lax.all_gather(query_weight, ("shard", "context"), axis=0, tiled=True),
        lax.all_gather(key_weight, ("shard", "context"), axis=0, tiled=True),
        lax.all_gather(value_weight, ("shard", "context"), axis=0, tiled=True),
        lax.all_gather(output_weight, ("shard", "context"), axis=0, tiled=True),
    )
    query = (jnp.dot(inputs, query_full, preferred_element_type=jnp.float32) + query_bias).astype(
        jnp.bfloat16
    )
    keys = jnp.dot(inputs, key_full, preferred_element_type=jnp.float32).astype(jnp.bfloat16)
    values = (jnp.dot(inputs, value_full, preferred_element_type=jnp.float32) + value_bias).astype(
        jnp.bfloat16
    )
    query_heads = query.reshape(rows, heads, DH)
    running_max = jnp.full((heads, rows), -jnp.inf, jnp.float32)
    running_sum = jnp.zeros((heads, rows), jnp.float32)
    accum = jnp.zeros((rows, width), jnp.float32)
    key_piece = lax.all_gather(keys, "context", axis=0, tiled=True)
    value_piece = lax.all_gather(values, "context", axis=0, tiled=True)
    count = key_piece.shape[0]
    scores = (
        jnp.einsum(
            "qhd,khd->hqk",
            query_heads,
            key_piece.reshape(count, heads, DH),
            preferred_element_type=jnp.float32,
        )
        * scale
    )
    new_max = jnp.max(scores, axis=2)
    exponent = jnp.exp(scores - new_max[:, :, None])
    decay = jnp.exp(running_max - new_max)
    new_sum = running_sum * decay + jnp.sum(exponent, axis=2)
    update = jnp.einsum(
        "hqk,khd->qhd",
        exponent.astype(jnp.bfloat16),
        value_piece.reshape(count, heads, DH),
        preferred_element_type=jnp.float32,
    )
    accum = accum.reshape(rows, heads, DH) * decay.T[:, :, None] + update
    top, total, accum = (new_max, new_sum, accum.reshape(rows, width))
    attended = (
        (accum.reshape(rows, heads, DH) / total.T[:, :, None])
        .reshape(rows, width)
        .astype(jnp.bfloat16)
    )
    logsum = top + jnp.log(total)
    attention_part = jnp.einsum(
        "tw,dw->td", attended, output_full, preferred_element_type=jnp.float32
    )
    first_sum = inputs.astype(jnp.float32) + forward_total(attention_part) + output_bias
    first_out, normed_one, inverse_one = layer_norm(first_sum, first_gain, first_shift)
    first_round = first_out.astype(jnp.bfloat16)
    up_full, down_full = (
        lax.all_gather(up_weight, ("shard", "context"), axis=0, tiled=True),
        lax.all_gather(down_weight, ("shard", "context"), axis=0, tiled=True),
    )
    up = jnp.dot(first_round, up_full, preferred_element_type=jnp.float32) + up_bias
    active = gelu_value(up).astype(jnp.bfloat16)
    mlp_part = jnp.einsum("tf,df->td", active, down_full, preferred_element_type=jnp.float32)
    second_sum = first_out + forward_total(mlp_part) + down_bias
    second_out, normed_two, inverse_two = layer_norm(second_sum, second_gain, second_shift)
    layer_output = second_out.astype(jnp.bfloat16)
    up_back, down_back = (
        lax.all_gather(up_weight, ("shard", "context"), axis=0, tiled=True),
        lax.all_gather(down_weight, ("shard", "context"), axis=0, tiled=True),
    )
    grad_out = cotangent[0].astype(jnp.float32)
    second_gain_part = jnp.sum(grad_out * normed_two, axis=0)
    second_shift_part = jnp.sum(grad_out, axis=0)
    back_two = norm_backward(grad_out, normed_two, inverse_two, second_gain)
    down_bias_part = jnp.sum(back_two, axis=0)
    back_two_round = back_two.astype(jnp.bfloat16)
    down_weight_part = jnp.einsum(
        "td,tf->df", back_two_round, active, preferred_element_type=jnp.float32
    )
    grad_up = jnp.dot(back_two_round, down_back, preferred_element_type=jnp.float32) * gelu_slope(
        up
    )
    up_bias_part = jnp.sum(grad_up, axis=0)
    up_round = grad_up.astype(jnp.bfloat16)
    up_weight_part = jnp.einsum(
        "td,tf->df", first_round, up_round, preferred_element_type=jnp.float32
    )
    mlp_grads = (
        scattered(up_weight_part),
        scattered(down_weight_part),
    )
    back_partial = jnp.einsum("tf,df->td", up_round, up_back, preferred_element_type=jnp.float32)
    back_one_in = backward_total(back_partial) + back_two
    first_gain_part = jnp.sum(back_one_in * normed_one, axis=0)
    first_shift_part = jnp.sum(back_one_in, axis=0)
    back_one = norm_backward(back_one_in, normed_one, inverse_one, first_gain)
    output_bias_part = jnp.sum(back_one, axis=0)
    back_one_round = back_one.astype(jnp.bfloat16)
    query_back, key_back, value_back, output_back = (
        lax.all_gather(query_weight, ("shard", "context"), axis=0, tiled=True),
        lax.all_gather(key_weight, ("shard", "context"), axis=0, tiled=True),
        lax.all_gather(value_weight, ("shard", "context"), axis=0, tiled=True),
        lax.all_gather(output_weight, ("shard", "context"), axis=0, tiled=True),
    )
    output_weight_part = jnp.einsum(
        "td,tw->dw", back_one_round, attended, preferred_element_type=jnp.float32
    )
    grad_attended = jnp.dot(back_one_round, output_back, preferred_element_type=jnp.float32).astype(
        jnp.bfloat16
    )
    grad_heads = grad_attended.reshape(rows, heads, DH)
    delta = jnp.sum(
        grad_heads.astype(jnp.float32) * attended.reshape(rows, heads, DH).astype(jnp.float32),
        axis=2,
    ).T

    def key_block(key_piece, value_piece):
        count = key_piece.shape[0]
        key_heads = key_piece.reshape(count, heads, DH)
        value_heads = value_piece.reshape(count, heads, DH)
        scores = (
            jnp.einsum("qhd,khd->hqk", query_heads, key_heads, preferred_element_type=jnp.float32)
            * scale
        )
        probs = jnp.exp(scores - logsum[:, :, None])
        grad_probs = jnp.einsum(
            "qhd,khd->hqk", grad_heads, value_heads, preferred_element_type=jnp.float32
        )
        grad_scores = (probs * (grad_probs - delta[:, :, None])).astype(jnp.bfloat16)
        value_term = jnp.einsum(
            "hqk,qhd->khd",
            probs.astype(jnp.bfloat16),
            grad_heads,
            preferred_element_type=jnp.float32,
        ).reshape(count, width)
        key_term = (
            jnp.einsum(
                "hqk,qhd->khd", grad_scores, query_heads, preferred_element_type=jnp.float32
            ).reshape(count, width)
            * scale
        )
        query_term = (
            jnp.einsum(
                "hqk,khd->qhd", grad_scores, key_heads, preferred_element_type=jnp.float32
            ).reshape(rows, width)
            * scale
        )
        return (query_term, key_term, value_term)

    first_query, first_key, first_value = key_block(keys, values)

    def turn(index, state):
        moving, grads_moving, query_accum = state
        moving = passed_along(moving, "context", 1)
        grads_moving = rotate_grads(grads_moving)
        query_term, key_term, value_term = key_block(moving[0], moving[1])
        return (moving, grads_moving + jnp.stack((key_term, value_term)), query_accum + query_term)

    moved, grads_moving, query_grad = lax.fori_loop(
        1,
        lax.axis_size("context"),
        turn,
        (jnp.stack((keys, values)), jnp.stack((first_key, first_value)), first_query),
    )
    returned = rotate_grads(grads_moving)
    key_grad, value_grad = (returned[0], returned[1])
    query_bias_part = jnp.sum(query_grad, axis=0)
    value_bias_part = jnp.sum(value_grad, axis=0)
    query_round = query_grad.astype(jnp.bfloat16)
    keys_round = key_grad.astype(jnp.bfloat16)
    values_round = value_grad.astype(jnp.bfloat16)
    query_weight_part = jnp.einsum(
        "td,tw->dw", inputs, query_round, preferred_element_type=jnp.float32
    )
    key_weight_part = jnp.einsum(
        "td,tw->dw", inputs, keys_round, preferred_element_type=jnp.float32
    )
    value_weight_part = jnp.einsum(
        "td,tw->dw", inputs, values_round, preferred_element_type=jnp.float32
    )
    attention_grads = (
        scattered(query_weight_part),
        scattered(key_weight_part),
        scattered(value_weight_part),
        scattered(output_weight_part),
    )
    input_partial = (
        jnp.einsum("tw,dw->td", query_round, query_back, preferred_element_type=jnp.float32)
        + jnp.einsum("tw,dw->td", keys_round, key_back, preferred_element_type=jnp.float32)
        + jnp.einsum("tw,dw->td", values_round, value_back, preferred_element_type=jnp.float32)
    )
    input_grad = backward_total(input_partial) + back_one
    small = lax.psum(
        (
            query_bias_part,
            value_bias_part,
            output_bias_part,
            first_gain_part,
            first_shift_part,
            up_bias_part,
            down_bias_part,
            second_gain_part,
            second_shift_part,
        ),
        ("shard", "context"),
    )
    return (
        layer_output[None],
        input_grad[None],
        attention_grads[0],
        attention_grads[1],
        attention_grads[2],
        attention_grads[3],
        small[0],
        small[1],
        small[2],
        small[3],
        small[4],
        mlp_grads[0],
        small[5],
        mlp_grads[1],
        small[6],
        small[7],
        small[8],
    )


def solution(mesh):
    placed = (
        P("shard", "context", None),
        P("shard", "context", None),
        P(("shard", "context"), "tensor"),
        P(("shard", "context"), "tensor"),
        P(("shard", "context"), "tensor"),
        P(("shard", "context"), "tensor"),
        P("tensor"),
        P("tensor"),
        P(),
        P(),
        P(),
        P(("shard", "context"), "tensor"),
        P("tensor"),
        P(("shard", "context"), "tensor"),
        P(),
        P(),
        P(),
    )
    return jax.shard_map(
        shards,
        mesh=mesh,
        in_specs=placed,
        out_specs=(
            P("shard", "context", None),
            P("shard", "context", None),
            P(("shard", "context"), "tensor"),
            P(("shard", "context"), "tensor"),
            P(("shard", "context"), "tensor"),
            P(("shard", "context"), "tensor"),
            P("tensor"),
            P("tensor"),
            P(),
            P(),
            P(),
            P(("shard", "context"), "tensor"),
            P("tensor"),
            P(("shard", "context"), "tensor"),
            P(),
            P(),
            P(),
        ),
        check_vma=False,
    )
```

```python
import functools

import jax
import jax.numpy as jnp
from jax import lax
from jax.experimental import pallas as pl
from jax.experimental.pallas import tpu as pltpu
from jax.sharding import PartitionSpec as P

DH = 64
TILE = 256
PARTS = 2

epsilon = 1e-05
root_half = 0.7071067811865476
inverse_root_two_pi = 0.3989422804014327

MESH = pl.DeviceIdType.MESH
BF = jnp.bfloat16
F32 = jnp.float32


def each(low, high, step):
    if high - low <= 4:
        for index in range(low, high):
            step(index)
    else:

        def run(index, carry):
            step(index)
            return carry

        lax.fori_loop(low, high, run, 0)


def looped(count, step):
    def run(index, carry):
        step(index)
        return carry

    lax.fori_loop(0, count, run, 0)


def dot_nn(left, right):
    return jnp.dot(left, right, preferred_element_type=F32)


def dot_nt(left, right):
    return lax.dot_general(left, right, (((1,), (1,)), ((), ())), preferred_element_type=F32)


def dot_tn(left, right):
    return lax.dot_general(left, right, (((0,), (0,)), ((), ())), preferred_element_type=F32)


def tile_of(extent):
    return TILE if extent % TILE == 0 else extent


def layer_norm(hidden):
    center = hidden - jnp.mean(hidden, axis=-1, keepdims=True)
    inverse = lax.rsqrt(jnp.mean(center * center, axis=-1, keepdims=True) + epsilon)
    return center * inverse, inverse


def norm_backward(grad, normed, inverse, gain):
    scaled = grad * gain
    return (
        scaled
        - jnp.mean(scaled, axis=-1, keepdims=True)
        - normed * jnp.mean(scaled * normed, axis=-1, keepdims=True)
    ) * inverse


def column_sum(values):
    return jnp.sum(values, axis=0, keepdims=True)


INPUTS = [
    "x", "cot", "wq", "wk", "wv", "wo", "bq", "bv", "bo",
    "g1", "s1", "wu", "bu", "wd", "bd", "g2", "s2",
]
OUTPUTS = [
    "oy", "ox", "oq", "ok", "ov", "oo", "obq", "obv", "obo",
    "og1", "os1", "ou", "obu", "od", "obd", "og2", "os2",
]


class Box:
    pass


def kernel(sizes, names, *refs):
    S, C, T, R, D, W, F = sizes
    N, H, CH = S * C, S // 2, (S // 2) * C
    Rb, Rt, Ru = D // N, R // (T * PARTS), R // PARTS
    heads = W // DH
    scale = DH ** (-0.5)
    r = Box()
    for name, ref in zip(names, refs):
        setattr(r, name, ref)

    s, c, t = lax.axis_index("shard"), lax.axis_index("context"), lax.axis_index("tensor")
    half, core = lax.div(s, 2), lax.rem(s, 2)
    other = 1 - core
    partner = (2 * half + other, c, t)
    chip = half * C + c
    own = s * C + c

    def chip_at(by):
        return lax.rem(chip + by, CH)

    def block_of(chip_index, core_index):
        return (2 * lax.div(chip_index, C) + core_index) * C + lax.rem(chip_index, C)

    def device_of(chip_index):
        return (2 * lax.div(chip_index, C) + core, lax.rem(chip_index, C), t)

    def rows_of(block, height):
        if isinstance(block, int):
            return pl.ds(block * height, height)
        return pl.ds(pl.multiple_of(block * height, height), height)

    def remote(src, dst, send, recv, device):
        return pltpu.make_async_remote_copy(
            src_ref=src, dst_ref=dst, send_sem=send, recv_sem=recv, device_id=device, device_id_type=MESH
        )

    pending = []

    def push(low, high, make):
        each(low, high, lambda p: make(p).start())
        pending.append((low, high, make))

    barrier = pltpu.get_barrier_semaphore()

    def plane_device(by):
        index = lax.rem(own + by, N)
        return (lax.div(index, C), lax.rem(index, C), t)

    def greet_plane(p):
        pl.semaphore_signal(barrier, inc=1, device_id=plane_device(p), device_id_type=MESH)

    def greet_tensor(p):
        pl.semaphore_signal(barrier, inc=1, device_id=(s, c, lax.rem(t + p, T)), device_id_type=MESH)

    each(1, N, greet_plane)
    each(1, T, greet_tensor)
    pl.semaphore_wait(barrier, N - 1 + T - 1)

    weights = (r.wq, r.wk, r.wv, r.wo, r.wu, r.wd)
    whole = (r.fq, r.fk, r.fv, r.fo, r.fu, r.fd)

    def gather_start(a):
        def across(p):
            rows = rows_of(own, Rb)
            return remote(weights[a], whole[a].at[rows], r.gs.at[a, p], r.gr.at[a, p], device_of(chip_at(p)))

        def aside(p):
            rows = rows_of(own, Rb)
            return remote(weights[a], whole[a].at[rows], r.fs.at[a, 0], r.fr.at[a, 0], partner)

        push(1, CH, across)
        push(0, 1, aside)
        pltpu.make_async_copy(weights[a], whole[a].at[rows_of(own, Rb)], r.ls.at[a]).start()

    def gather_forward(a):
        def arrived(p):
            rows = rows_of(block_of(chip_at(CH - p), core), Rb)
            piece = whole[a].at[rows]
            remote(piece, piece, r.gs.at[a, p], r.gr.at[a, p], partner).wait_recv()

        def onward(p):
            rows = rows_of(block_of(chip_at(CH - p), core), Rb)
            piece = whole[a].at[rows]
            return remote(piece, piece, r.fs.at[a, p], r.fr.at[a, p], partner)

        def both(p):
            arrived(p)
            onward(p).start()

        each(1, CH, both)
        pending.append((1, CH, onward))

    def gather_finish(a):
        pltpu.make_async_copy(weights[a], whole[a].at[rows_of(own, Rb)], r.ls.at[a]).wait()

        def landed(p):
            rows = rows_of(block_of(chip_at(CH - p), other), Rb)
            piece = whole[a].at[rows]
            remote(piece, piece, r.fs.at[a, p], r.fr.at[a, p], partner).wait_recv()

        each(0, CH, landed)

    parts = range(PARTS)

    def sum_start(k, u):
        def make(p):
            to = lax.rem(t + p, T)
            return remote(
                r.zs.at[k, rows_of(u * T + to, Rt)],
                r.zr.at[k, u, p - 1],
                r.zss.at[k * PARTS + u, p - 1],
                r.zrs.at[k * PARTS + u, p - 1],
                (s, c, to),
            )

        push(1, T, make)

    def sum_finish(k, u):
        total = r.zs[k, rows_of(u * T + t, Rt), :].astype(F32)
        for p in range(1, T):
            piece = r.zr.at[k, u, p - 1]
            remote(
                piece, piece, r.zss.at[k * PARTS + u, p - 1], r.zrs.at[k * PARTS + u, p - 1], (s, c, t)
            ).wait_recv()
            total = total + r.zr[k, u, p - 1].astype(F32)
        return total

    def copy_start(k, u):
        def make(p):
            piece = r.ag.at[k, rows_of(u * T + t, Rt)]
            return remote(
                piece,
                piece,
                r.ass.at[k * PARTS + u, p - 1],
                r.ars.at[k * PARTS + u, p - 1],
                (s, c, lax.rem(t + p, T)),
            )

        push(1, T, make)

    def copy_finish(k, u):
        for p in range(1, T):
            piece = r.ag.at[k, rows_of(u * T + lax.rem(t + T - p, T), Rt)]
            remote(
                piece, piece, r.ass.at[k * PARTS + u, p - 1], r.ars.at[k * PARTS + u, p - 1], (s, c, t)
            ).wait_recv()

    grads = tuple((r.da.at[a], r.pa.at[a], r.ta.at[a], r.ra.at[a]) for a in range(4)) + tuple(
        (r.df.at[a], r.pf.at[a], r.tf.at[a], r.rf.at[a]) for a in range(2)
    )
    results = (r.oq, r.ok, r.ov, r.oo, r.ou, r.od)

    def scatter_aside(a):
        part, aside, _, _ = grads[a]

        def make(h):
            return remote(
                part.at[rows_of(2 * h + other, C * Rb)], aside.at[h], r.ps.at[a, h], r.pr.at[a, h], partner
            )

        push(0, H, make)

    def scatter_across(a):
        part, aside, sums, landing = grads[a]

        def add(h):
            piece = aside.at[h]
            remote(piece, piece, r.ps.at[a, h], r.pr.at[a, h], partner).wait_recv()
            mine = part[rows_of(2 * h + core, C * Rb), :].astype(F32)
            sums[h, :, :] = (mine + aside[h].astype(F32)).astype(BF)

        each(0, H, add)

        def make(p):
            to = chip_at(p)
            return remote(
                sums.at[lax.div(to, C), rows_of(lax.rem(to, C), Rb)],
                landing.at[p - 1],
                r.ts.at[a, p - 1],
                r.tr.at[a, p - 1],
                device_of(to),
            )

        push(1, CH, make)

    def scatter_finish(a):
        part, aside, _, landing = grads[a]
        own_rows = rows_of(own, Rb)
        results[a][...] = part[own_rows, :].astype(F32) + aside[half, rows_of(c, Rb), :].astype(F32)

        def add(p):
            piece = landing.at[p - 1]
            remote(piece, piece, r.ts.at[a, p - 1], r.tr.at[a, p - 1], partner).wait_recv()
            results[a][...] = results[a][...] + landing[p - 1].astype(F32)

        each(1, CH, add)

    def weight_grad(target, left, right):
        block = tile_of(D)

        def step(i):
            rows = rows_of(i, block)
            target[rows, :] = dot_tn(left[:, rows], right[...]).astype(BF)

        looped(D // block, step)

    def to_features(k, u, pairs):
        block = tile_of(D)
        part = rows_of(u, Ru)

        def step(i):
            rows = rows_of(i, block)
            total = dot_nt(pairs[0][0][part, :], pairs[0][1][rows, :])
            for left, right in pairs[1:]:
                total = total + dot_nt(left[part, :], right[rows, :])
            r.zs[k, part, rows] = total.astype(BF)

        looped(D // block, step)

    for a in (1, 2, 0):
        gather_start(a)
    x = r.x[...]
    gather_forward(1)
    gather_finish(1)
    own_context = rows_of(c, R)
    r.ka[own_context, :] = dot_nn(x, r.fk[...]).astype(BF)

    def context_copy(buffer, send, recv):
        def make(p):
            piece = buffer.at[rows_of(c, R)]
            return remote(piece, piece, send.at[p - 1], recv.at[p - 1], (s, lax.rem(c + p, C), t))

        push(1, C, make)

    def context_arrived(buffer, send, recv):
        def arrived(p):
            piece = buffer.at[rows_of(lax.rem(c + C - p, C), R)]
            remote(piece, piece, send.at[p - 1], recv.at[p - 1], (s, c, t)).wait_recv()

        each(1, C, arrived)

    context_copy(r.ka, r.ks, r.kr)
    gather_forward(2)
    gather_finish(2)
    r.va[own_context, :] = (dot_nn(x, r.fv[...]) + r.bv[...]).astype(BF)
    context_copy(r.va, r.vs, r.vr)
    gather_forward(0)
    gather_start(3)
    gather_start(4)
    gather_start(5)
    gather_finish(0)
    r.q[...] = (dot_nn(x, r.fq[...]) + r.bq[...]).astype(BF)
    context_arrived(r.ka, r.ks, r.kr)
    context_arrived(r.va, r.vs, r.vr)

    lanes = lax.broadcasted_iota(jnp.int32, (1, W), 1)

    def head_mask(h):
        return jnp.where((lanes >= h * DH) & (lanes < h * DH + DH), 1.0, 0.0)

    r.acc[...] = jnp.zeros_like(r.acc)

    def head_forward(h):
        mask = head_mask(h)
        scores = dot_nt(r.q[...] * mask.astype(BF), r.ka[...]) * scale
        top = jnp.max(scores, axis=1, keepdims=True)
        exponent = jnp.exp(scores - top)
        total = jnp.sum(exponent, axis=1, keepdims=True)
        mixed = dot_nn(exponent.astype(BF), r.va[...]) / total
        r.acc[...] = r.acc[...] + mixed * mask
        r.lse[h] = top + jnp.log(total)

    looped(heads // 2, head_forward)
    gather_forward(3)
    looped(heads - heads // 2, lambda h: head_forward(heads // 2 + h))
    r.att[...] = r.acc[...].astype(BF)
    gather_finish(3)
    for u in parts:
        to_features(0, u, ((r.att, r.fo),))
        sum_start(0, u)
    gather_forward(4)
    for u in parts:
        token_rows, kept = rows_of(u * T + t, Rt), rows_of(u, Rt)
        first_sum = r.x[token_rows, :].astype(F32) + sum_finish(0, u) + r.bo[...]
        normed_one, inverse_one = layer_norm(first_sum)
        first_out = normed_one * r.g1[...] + r.s1[...]
        r.ag[0, token_rows, :] = first_out.astype(BF)
        copy_start(0, u)
        r.n1[kept, :] = normed_one
        r.i1[kept, :] = inverse_one
        r.f1[kept, :] = first_out
    gather_finish(4)
    gather_forward(5)
    block = tile_of(F)
    for u in parts:
        part = rows_of(u, Ru)
        copy_finish(0, u)

        def up_step(i):
            columns = rows_of(i, block)
            up = dot_nn(r.ag[0, part, :], r.fu[:, columns]) + r.bu[:, columns]
            r.up[part, columns] = up
            r.act[part, columns] = (0.5 * up * (1.0 + lax.erf(up * root_half))).astype(BF)

        looped(F // block, up_step)
        if u == 0:
            gather_finish(5)
        to_features(1, u, ((r.act, r.fd),))
        sum_start(1, u)

    def slope_step(i):
        columns = rows_of(i, block)
        up = r.up[:, columns]
        r.up[:, columns] = 0.5 * (1.0 + lax.erf(up * root_half)) + up * inverse_root_two_pi * jnp.exp(
            -0.5 * up * up
        )

    looped(F // block, slope_step)
    sums = [0.0, 0.0, 0.0]
    for u in parts:
        token_rows, kept = rows_of(u * T + t, Rt), rows_of(u, Rt)
        second_sum = r.f1[kept, :] + sum_finish(1, u) + r.bd[...]
        normed_two, inverse_two = layer_norm(second_sum)
        grad_out = r.cot[token_rows, :].astype(F32)
        back_two = norm_backward(grad_out, normed_two, inverse_two, r.g2[...])
        r.ag[1, token_rows, :] = back_two.astype(BF)
        copy_start(1, u)
        r.b2[kept, :] = back_two
        r.ag[3, token_rows, :] = (normed_two * r.g2[...] + r.s2[...]).astype(BF)
        sums[0] += column_sum(back_two)
        sums[1] += column_sum(grad_out * normed_two)
        sums[2] += column_sum(grad_out)
    for row in range(3):
        r.st[t, 3 + row : 4 + row, :] = sums[row]
    r.st[t, 6:8, :] = jnp.zeros((2, D), F32)
    for u in parts:
        part = rows_of(u, Ru)
        copy_finish(1, u)

        def down_step(i):
            columns = rows_of(i, block)
            grad_up = dot_nn(r.ag[1, part, :], r.fd[:, columns]) * r.up[part, columns]
            total = column_sum(grad_up)
            if u > 0:
                total = total + r.sp[own, 6:7, columns]
            r.sp[own, 6:7, columns] = total
            r.gu[part, columns] = grad_up.astype(BF)

        looped(F // block, down_step)
        to_features(2, u, ((r.gu, r.fu),))
        sum_start(2, u)
    weight_grad(r.df.at[1], r.ag.at[1], r.act)
    scatter_aside(5)
    weight_grad(r.df.at[0], r.ag.at[0], r.gu)
    scatter_aside(4)
    scatter_across(5)
    sums = [0.0, 0.0, 0.0]
    for u in parts:
        token_rows, kept = rows_of(u * T + t, Rt), rows_of(u, Rt)
        back_one_in = sum_finish(2, u) + r.b2[kept, :]
        normed_one = r.n1[kept, :]
        back_one = norm_backward(back_one_in, normed_one, r.i1[kept, :], r.g1[...])
        r.ag[2, token_rows, :] = back_one.astype(BF)
        copy_start(2, u)
        r.b1[kept, :] = back_one
        sums[0] += column_sum(back_one)
        sums[1] += column_sum(back_one_in * normed_one)
        sums[2] += column_sum(back_one_in)
    scatter_across(4)
    for row in range(3):
        r.st[t, row : 1 + row, :] = sums[row]

    def small_tensor(p):
        piece = r.st.at[t]
        return remote(piece, piece, r.sts.at[p - 1], r.str.at[p - 1], (s, c, lax.rem(t + p, T)))

    push(1, T, small_tensor)
    for u in parts:
        copy_start(3, u)

    for u in parts:
        part = rows_of(u, Ru)
        copy_finish(2, u)
        r.ga[part, :] = dot_nn(r.ag[2, part, :], r.fo[...]).astype(BF)
    r.acc[...] = jnp.zeros_like(r.acc)
    r.dk[...] = jnp.zeros_like(r.dk)
    r.dv[...] = jnp.zeros_like(r.dv)

    keys_block = 2 * R if C % 2 == 0 else R

    def head_backward(h):
        mask = head_mask(h)
        mask_bf = mask.astype(BF)
        grad_head = r.ga[...] * mask_bf
        delta = jnp.sum(grad_head.astype(F32) * r.att[...].astype(F32), axis=1, keepdims=True)
        query_head = r.q[...] * mask_bf

        def key_block(i):
            rows = rows_of(i, keys_block)
            scores = dot_nt(query_head, r.ka[rows, :]) * scale
            probs = jnp.exp(scores - r.lse[h])
            grad_probs = dot_nt(grad_head, r.va[rows, :])
            grad_scores = (probs * (grad_probs - delta)).astype(BF)
            r.dv[rows, :] = r.dv[rows, :] + dot_tn(probs.astype(BF), grad_head)
            r.dk[rows, :] = r.dk[rows, :] + dot_tn(grad_scores, query_head) * scale
            r.acc[...] = r.acc[...] + dot_nn(grad_scores, r.ka[rows, :]) * (mask * scale)

        each(0, C * R // keys_block, key_block)

    looped(heads, head_backward)
    r.kb[0] = r.dk[...].astype(BF)
    r.kb[1] = r.dv[...].astype(BF)

    def key_grads(p):
        to = lax.rem(c + p, C)
        return remote(
            r.kb.at[:, rows_of(to, R)], r.kc.at[p - 1], r.cs.at[p - 1], r.cr.at[p - 1], (s, to, t)
        )

    push(1, C, key_grads)
    query_grad = r.acc[...]
    r.qr[...] = query_grad.astype(BF)
    r.sp[own, 7:8, 0:W] = column_sum(query_grad)
    weight_grad(r.da.at[3], r.ag.at[2], r.att)
    scatter_aside(3)
    weight_grad(r.da.at[0], r.x, r.qr)
    scatter_aside(0)
    scatter_across(3)
    scatter_across(0)

    def add_keys(p):
        piece = r.kc.at[p - 1]
        remote(piece, piece, r.cs.at[p - 1], r.cr.at[p - 1], (s, c, t)).wait_recv()
        r.dk[own_context, :] = r.dk[own_context, :] + r.kc[p - 1, 0].astype(F32)
        r.dv[own_context, :] = r.dv[own_context, :] + r.kc[p - 1, 1].astype(F32)

    each(1, C, add_keys)
    r.kr2[...] = r.dk[own_context, :].astype(BF)
    value_grad = r.dv[own_context, :]
    r.vr2[...] = value_grad.astype(BF)
    r.sp[own, 7:8, W : 2 * W] = column_sum(value_grad)
    for u in parts:
        to_features(3, u, ((r.qr, r.fq), (r.kr2, r.fk), (r.vr2, r.fv)))
        sum_start(3, u)
    weight_grad(r.da.at[1], r.x, r.kr2)
    scatter_aside(1)
    weight_grad(r.da.at[2], r.x, r.vr2)
    scatter_aside(2)

    for p in range(1, T):
        piece = r.st.at[t]
        remote(piece, piece, r.sts.at[p - 1], r.str.at[p - 1], (s, c, t)).wait_recv()
    small = r.st[0]
    for index in range(1, T):
        small = small + r.st[index]
    r.sp[own, 0:6, 0:D] = small[0:6]

    def small_plane(p):
        piece = r.sp.at[own]
        return remote(piece, piece, r.sps.at[p - 1], r.spr.at[p - 1], plane_device(p))

    push(1, N, small_plane)
    scatter_across(1)
    scatter_across(2)
    for u in parts:
        r.ag[4, rows_of(u * T + t, Rt), :] = (sum_finish(3, u) + r.b1[rows_of(u, Rt), :]).astype(BF)
        copy_start(4, u)
    scatter_finish(5)
    scatter_finish(4)
    scatter_finish(3)
    scatter_finish(0)
    for u in parts:
        copy_finish(3, u)
    r.oy[...] = r.ag[3]

    def small_arrived(p):
        piece = r.sp.at[own]
        remote(piece, piece, r.sps.at[p - 1], r.spr.at[p - 1], (s, c, t)).wait_recv()

    each(1, N, small_arrived)
    total = r.sp[0]
    for index in range(1, N):
        total = total + r.sp[index]
    for row, ref in enumerate((r.obo, r.og1, r.os1, r.obd, r.og2, r.os2)):
        ref[...] = total[row : row + 1, 0:D]
    r.obu[...] = total[6:7, 0:F]
    r.obq[...] = total[7:8, 0:W]
    r.obv[...] = total[7:8, W : 2 * W]
    for u in parts:
        copy_finish(4, u)
    r.ox[...] = r.ag[4].astype(F32)
    scatter_finish(1)
    scatter_finish(2)
    for low, high, make in pending:
        each(low, high, lambda p: make(p).wait_send())


def shards(sizes, *args):
    S, C, T = sizes
    tokens, wq, wu = args[0], args[2], args[11]
    R, D = tokens.shape[1:]
    W, F = wq.shape[1], wu.shape[1]
    N, H, CH = S * C, S // 2, (S // 2) * C
    Rb, Rt, M = D // N, R // (T * PARTS), max(D, F)
    Rp = PARTS * Rt
    heads = W // DH
    operands, in_specs = [], []
    for name, arg in zip(INPUTS, args):
        if arg.ndim == 3:
            arg = arg[0]
        if arg.ndim == 1:
            arg = arg[None]
        operands.append(arg)
        space = pl.ANY if name[0] == "w" else pltpu.VMEM
        in_specs.append(pl.BlockSpec(memory_space=space))
    wide, narrow = (1, D), (1, W)
    out_shapes = [
        ((R, D), BF),
        ((R, D), F32),
        ((Rb, W), F32),
        ((Rb, W), F32),
        ((Rb, W), F32),
        ((Rb, W), F32),
        (narrow, F32),
        (narrow, F32),
        (wide, F32),
        (wide, F32),
        (wide, F32),
        ((Rb, F), F32),
        ((1, F), F32),
        ((Rb, F), F32),
        (wide, F32),
        (wide, F32),
        (wide, F32),
    ]
    peers = max(CH - 1, 1)
    ring = max(C - 1, 1)
    scratch = {
        "fq": ((D, W), BF),
        "fk": ((D, W), BF),
        "fv": ((D, W), BF),
        "fo": ((D, W), BF),
        "fu": ((D, F), BF),
        "fd": ((D, F), BF),
        "ka": ((C * R, W), BF),
        "va": ((C * R, W), BF),
        "q": ((R, W), BF),
        "acc": ((R, W), F32),
        "lse": ((heads, R, 1), F32),
        "att": ((R, W), BF),
        "zs": ((4, R, D), BF),
        "zr": ((4, PARTS, T - 1, Rt, D), BF),
        "ag": ((5, R, D), BF),
        "n1": ((Rp, D), F32),
        "i1": ((Rp, 1), F32),
        "f1": ((Rp, D), F32),
        "b2": ((Rp, D), F32),
        "b1": ((Rp, D), F32),
        "up": ((R, F), F32),
        "act": ((R, F), BF),
        "gu": ((R, F), BF),
        "ga": ((R, W), BF),
        "dk": ((C * R, W), F32),
        "dv": ((C * R, W), F32),
        "kb": ((2, C * R, W), BF),
        "kc": ((ring, 2, R, W), BF),
        "qr": ((R, W), BF),
        "kr2": ((R, W), BF),
        "vr2": ((R, W), BF),
        "da": ((4, D, W), BF),
        "pa": ((4, H, C * Rb, W), BF),
        "ta": ((4, H, C * Rb, W), BF),
        "ra": ((4, peers, Rb, W), BF),
        "df": ((2, D, F), BF),
        "pf": ((2, H, C * Rb, F), BF),
        "tf": ((2, H, C * Rb, F), BF),
        "rf": ((2, peers, Rb, F), BF),
        "st": ((T, 8, D), F32),
        "sp": ((N, 8, M), F32),
    }
    semaphores = {
        "gs": (6, CH),
        "gr": (6, CH),
        "fs": (6, CH),
        "fr": (6, CH),
        "ls": (6,),
        "zss": (4 * PARTS, T - 1),
        "zrs": (4 * PARTS, T - 1),
        "ass": (5 * PARTS, T - 1),
        "ars": (5 * PARTS, T - 1),
        "ps": (6, H),
        "pr": (6, H),
        "ts": (6, peers),
        "tr": (6, peers),
        "ks": (ring,),
        "kr": (ring,),
        "vs": (ring,),
        "vr": (ring,),
        "cs": (ring,),
        "cr": (ring,),
        "sts": (T - 1,),
        "str": (T - 1,),
        "sps": (N - 1,),
        "spr": (N - 1,),
    }
    names = INPUTS + OUTPUTS + list(scratch) + list(semaphores)
    outs = pl.pallas_call(
        functools.partial(kernel, (S, C, T, R, D, W, F), names),
        out_shape=[jax.ShapeDtypeStruct(shape, dtype) for shape, dtype in out_shapes],
        in_specs=in_specs,
        out_specs=[pl.BlockSpec(memory_space=pltpu.VMEM)] * len(out_shapes),
        scratch_shapes=[pltpu.VMEM(shape, dtype) for shape, dtype in scratch.values()]
        + [pltpu.SemaphoreType.DMA(shape) for shape in semaphores.values()],
        compiler_params=pltpu.CompilerParams(
            collective_id=0, has_side_effects=True, vmem_limit_bytes=62 * 1024 * 1024
        ),
    )(*operands)
    shaped = []
    for index, out in enumerate(outs):
        if index < 2:
            out = out[None]
        elif out.shape[0] == 1:
            out = out[0]
        shaped.append(out)
    return tuple(shaped)


def solution(mesh):
    rows = P("shard", "context", None)
    weight = P(("shard", "context"), "tensor")
    cut, same = P("tensor"), P()
    sizes = tuple(mesh.shape[name] for name in ("shard", "context", "tensor"))
    return jax.shard_map(
        functools.partial(shards, sizes),
        mesh=mesh,
        in_specs=(
            (rows, rows) + (weight,) * 4 + (cut, cut, same, same, same, weight, cut, weight, same, same, same)
        ),
        out_specs=(
            (rows, rows) + (weight,) * 4 + (cut, cut, same, same, same, weight, cut, weight, same, same, same)
        ),
        check_vma=False,
    )
```
